768 devices in a mesh: row: 192 (over z, y, core), col: 4 (over x).
Axes of the slice: x: 4, y: 8, z: 12, core: 2. Of those that a mesh axis runs over, the one named last changes fastest.
Arguments:
- amplitudes: bfloat16 [24576, 128], P(('row', 'col')), may hold values from -6 to 6
- driver: bfloat16 [24576, 128], P(('row', 'col')), may hold values from -6 to 6
- ladder_integrals: bfloat16 [4, 6144, 6144], P('col', 'row'), as said below
- cycle_kernel: bfloat16 [192, 4, 64, 12288], P('row', 'col'), may hold values from -0.0546875 to 0.0546875
- cycle_target: int32 [24576], P(('row', 'col')), may hold values from 0 to 63, as said below
- vir_energy: float32 [24576], P(('row', 'col')), may hold values from 1 to 4
- occ_energy: float32 [128], replicated, may hold values from -2 to -0.5
Outputs:
- update: float32 [24576, 128], P(('row', 'col'))
The draws below stay inside these ranges and needn't reach their ends.
Inputs may be any that keep to these rules, and one draw needn't show every extreme that they name: ladder_integrals[c] is a symmetric matrix for every c. `cycle_target`: within the 32 pairs of one tile the values are distinct; value // 16 is an owner among the tiles of the same first index and value % 16 a slot. Every tile sends exactly 16 pairs to one owner, the same owner for all tiles of one first index; the rest go to the other owners.
All inputs are finite; a program needn't handle non-finite values.
Results may differ from the reference program's by a relative error of at most 0.00084.
Values may be sent and summed in bfloat16 or wider, within the bound.
A program may use at most 32 MiB of HBM per device.

```python
import math
import jax
import jax.numpy as jnp
from jax import lax

PAIR_DEV = 32
OCC_PAIRS = 128
CAPACITY = 16
CYCLE_ROWS = 64
CYCLE_WIDTH = 12288
PAIRS_COL = 6144
VPAIRS = 24576
N_ROW = 192
N_COL = 4


def draw_ladder_integrals(key, part):

    def one_column(column):
        sub_key = jax.random.fold_in(key, column)
        base = jax.random.normal(sub_key, (PAIRS_COL, PAIRS_COL), jnp.float32)
        return ((base + base.T) * jnp.sqrt(2.0 / PAIRS_COL)).astype(jnp.bfloat16)
    return lax.map(one_column, jnp.arange(N_COL, dtype=jnp.int32))


def draw_cycle_target(key, part):
    tile_count = VPAIRS // PAIR_DEV
    row_count = tile_count // N_COL
    key_heavy = jax.random.fold_in(key, 11)
    key_tiles = jax.random.fold_in(key, 23)
    heavy_rows = jax.random.randint(key_heavy, (row_count,), 0, N_COL)
    heavy_tiles = jnp.repeat(heavy_rows, N_COL)
    tile_keys = jax.random.split(key_tiles, tile_count)

    def one_tile(tile_key, heavy):
        key_first = jax.random.fold_in(tile_key, 1)
        key_second = jax.random.fold_in(tile_key, 2)
        key_third = jax.random.fold_in(tile_key, 3)
        heavy_slots = jax.random.permutation(key_first, CAPACITY).astype(jnp.int32)
        heavy_values = heavy * CAPACITY + heavy_slots
        others = jax.random.permutation(key_second, (N_COL - 1) * CAPACITY).astype(jnp.int32)
        others = others[:PAIR_DEV - CAPACITY]
        other_index = others // CAPACITY
        owner = other_index + (other_index >= heavy).astype(jnp.int32)
        other_values = owner * CAPACITY + others % CAPACITY
        values = jnp.concatenate([heavy_values, other_values])
        order = jax.random.permutation(key_third, PAIR_DEV)
        return values[order]
    result = jax.vmap(one_tile)(tile_keys, heavy_tiles)
    return result.reshape(tile_count * PAIR_DEV).astype(jnp.int32)


def levels(key, shape, cuts, smallest, top_value):
    def one(dim, blocks):
        steps = jax.random.uniform(jax.random.fold_in(jax.random.fold_in(key, 6), dim), (blocks,), jnp.float32, smallest / len(cuts), top_value / len(cuts))
        return jnp.repeat(jnp.exp(steps), shape[dim] // blocks).reshape((-1,) + (1,) * (len(shape) - dim - 1))

    gain = one(*cuts[0])
    for cut in cuts[1:]:
        gain = gain * one(*cut)
    return gain


def scatter_about(key, shape, spread, limit, cuts=(), kind=jnp.bfloat16):
    array = spread * jax.random.normal(key, shape, jnp.float32)
    if cuts:
        array = array * levels(key, shape, cuts, -0.22, 0.18)
    return jnp.clip(array, -limit, limit).astype(kind)


def setup_inputs(seed: int = 0) -> dict:
    key_of = jax.random.split(jax.random.key(seed), 8)
    return {
        "amplitudes": scatter_about(key_of[0], (VPAIRS, OCC_PAIRS), 1.0, 6.0, ((0, 768),)),
        "driver": scatter_about(key_of[1], (VPAIRS, OCC_PAIRS), 1.0, 6.0, ((0, 768),)),
        "ladder_integrals": draw_ladder_integrals(jax.random.fold_in(key_of[7], 71), 0),
        "cycle_kernel": scatter_about(key_of[3], (N_ROW, N_COL, CYCLE_ROWS, CYCLE_WIDTH), CYCLE_WIDTH ** -0.5, 0.0546875, ((0, 192), (1, 4))),
        "cycle_target": draw_cycle_target(jax.random.fold_in(key_of[7], 71), 0),
        "vir_energy": jnp.clip(jnp.exp(math.log(4.0) - 1.3862944 * jax.random.uniform(key_of[5], (VPAIRS,), jnp.float32) ** levels(key_of[5], (VPAIRS,), ((0, 768),), -0.2, 0.2)), 1.0, 4.0),
        "occ_energy": jnp.clip(jax.random.uniform(key_of[6], (OCC_PAIRS,), jnp.float32, -2.0, -0.5), -2.0, -0.5),
    }


def reference(amplitudes, driver, ladder_integrals, cycle_kernel, cycle_target, vir_energy, occ_energy):
    blocks = amplitudes.reshape(N_ROW, N_COL, PAIR_DEV, OCC_PAIRS)

    def ladder_one(packed):
        integrals, column_amps = packed
        flat = column_amps.reshape(N_ROW * PAIR_DEV, OCC_PAIRS)
        result = jnp.dot(integrals, flat, preferred_element_type=jnp.float32)
        return result.reshape(N_ROW, PAIR_DEV, OCC_PAIRS)

    ladder = lax.map(ladder_one, (ladder_integrals, jnp.swapaxes(blocks, 0, 1)))
    ladder = jnp.swapaxes(ladder, 0, 1)

    targets = cycle_target.reshape(N_ROW, N_COL, PAIR_DEV)
    slot_ids = jnp.arange(N_COL * CAPACITY, dtype=jnp.int32)

    def place_one(packed):
        row_amps, target = packed
        onehot = (target[:, :, None] == slot_ids[None, None, :]).astype(jnp.float32)
        placed = jnp.einsum("ckm,cko->mco", onehot, row_amps.astype(jnp.float32))
        tiles = placed.reshape(N_COL, CAPACITY, N_COL, OCC_PAIRS).transpose(0, 2, 1, 3)
        return tiles.reshape(N_COL, CYCLE_ROWS, OCC_PAIRS)

    cycle_tiles = lax.map(place_one, (blocks, targets))
    by_owner = jnp.swapaxes(cycle_tiles, 0, 1).reshape(N_COL, N_ROW * CYCLE_ROWS, OCC_PAIRS)

    def mix_one(kernels):
        mixed = jnp.einsum("gpq,gqo->gpo", kernels.astype(jnp.float32), by_owner)
        rounded = lax.optimization_barrier(mixed.astype(jnp.bfloat16))
        return rounded.astype(jnp.float32)

    cycle_mixed = lax.map(mix_one, cycle_kernel)

    def return_one(packed):
        target, mixed = packed
        onehot = (target[:, :, None] == slot_ids[None, None, :]).astype(jnp.float32)
        returned = mixed.reshape(N_COL, N_COL, CAPACITY, OCC_PAIRS).transpose(1, 0, 2, 3)
        returned = returned.reshape(N_COL, CYCLE_ROWS, OCC_PAIRS)
        return jnp.einsum("ckm,cmo->cko", onehot, returned)

    cycle_term = lax.map(return_one, (targets, cycle_mixed))
    summed = driver.reshape(N_ROW, N_COL, PAIR_DEV, OCC_PAIRS).astype(jnp.float32) + ladder + cycle_term
    denominator = vir_energy.reshape(N_ROW, N_COL, PAIR_DEV)[..., None] - occ_energy[None, None, None, :]
    return (summed / denominator).reshape(N_ROW * N_COL * PAIR_DEV, OCC_PAIRS)
```

```python
import functools

import jax
import jax.numpy as jnp
from jax import lax
from jax.experimental import pallas as pl
from jax.experimental.pallas import tpu as pltpu
from jax.sharding import Mesh
from jax.sharding import PartitionSpec as P

ROW = ("row_0", "row_1", "row_2")
ROW_COL = ("row_0", "row_1", "row_2", "col")
MESH = pl.DeviceIdType.MESH
CORES = 2


def fused(
    nz, ny, nx, amp_ref, tgt_ref, ladder_hbm, cycle_hbm, out_ref,
    gath, ladder_v, cycle_v, placed, mix, ret,
    w_sem, ring_send, first_recv, second_recv, part_send, part_recv,
    x_send, x_recv, back_send, back_recv,
):
    z, y, core, x = (lax.axis_index(a) for a in ROW_COL)
    pair, occ = amp_ref.shape
    cap = placed.shape[1]
    crow = nx * cap
    blocks = nz * ny

    load_l = pltpu.make_async_copy(ladder_hbm, ladder_v, w_sem.at[0])
    load_c = pltpu.make_async_copy(cycle_hbm, cycle_v, w_sem.at[1])
    load_l.start()
    load_c.start()

    def at(dz=0, dy=0, dx=0, dc=0):
        return (
            lax.rem(z + dz + nz, nz), lax.rem(y + dy + ny, ny),
            lax.rem(core + dc, CORES), lax.rem(x + dx, nx),
        )

    barrier = pltpu.get_barrier_semaphore()
    peers = [at(dz=1), at(dz=-1), at(dy=1), at(dy=-1), at(dc=1)]
    peers += [at(dx=j) for j in range(1, nx)]
    for peer in peers:
        pl.semaphore_signal(barrier, inc=1, device_id=peer, device_id_type=MESH)

    slot_ids = lax.broadcasted_iota(jnp.int32, (crow, pair), 0)
    onehot = (slot_ids == tgt_ref[...]).astype(jnp.float32).astype(jnp.bfloat16)
    own = jnp.dot(onehot, amp_ref[...], preferred_element_type=jnp.float32)
    placed[...] = own.astype(jnp.bfloat16).reshape(nx, cap, occ)

    my_slot = jnp.where(core == 0, z * ny + y, y * nz + z)
    gath[core, my_slot, pl.ds(0, pair), :] = amp_ref[...]
    my_part = pl.ds(pl.multiple_of(pair + x * cap, cap), cap)
    gath[core, my_slot, my_part, :] = placed[x]

    pl.semaphore_wait(barrier, len(peers))

    def remote(src, dst, send_sem, recv_sem, device):
        return pltpu.make_async_remote_copy(
            src_ref=src, dst_ref=dst, send_sem=send_sem, recv_sem=recv_sem,
            device_id=device, device_id_type=MESH,
        )

    def out_x(j):
        to = at(dx=j)
        return remote(
            placed.at[to[3]], gath.at[core, my_slot, my_part, :], x_send.at[j], x_recv.at[j], to
        )

    for j in range(1, nx):
        out_x(j).start()
    for j in range(1, nx):
        out_x(j).wait_recv()

    partner = at(dc=1)

    def plane(p):
        n1, n2 = (ny, nz) if p == 0 else (nz, ny)
        i1, i2 = (y, z) if p == 0 else (z, y)
        first = [at(dy=1), at(dy=-1)] if p == 0 else [at(dz=1), at(dz=-1)]
        second = [at(dz=1), at(dz=-1)] if p == 0 else [at(dy=1), at(dy=-1)]

        def block(a2, a1):
            return gath.at[p, lax.rem(a2 + 2 * n2, n2) * n1 + lax.rem(a1 + 2 * n1, n1)]

        def ring(src, recv_sem, device):
            return remote(src, src, ring_send, recv_sem, device)

        def to_partner(src):
            remote(src, src, part_send, part_recv, partner).start()

        def launch(k, src):
            for d in range(2):
                ring(src, second_recv.at[d, k * (n2 // 2)], second[d]).start()
            to_partner(src)

        def step(t, carry):
            def column(k, carry):
                s1 = (k + 1) // 2
                down = lax.rem(k + 1, 2)
                j = jnp.where(down == 0, i1 - s1, i1 + s1)

                @pl.when(t == s1)
                def _():
                    src = block(i2, j)
                    for d in range(2):

                        @pl.when((k > 0) & (down == d))
                        def _():
                            ring(src, first_recv.at[d, s1 - 1], first[d]).wait_recv()

                            @pl.when(k + 2 < n1)
                            def _():
                                ring(src, first_recv.at[d, s1], first[d]).start()

                    @pl.when(k == 0)
                    def _():
                        for d in range(2):
                            ring(src, first_recv.at[d, 0], first[d]).start()

                    launch(k, src)

                s2 = t - s1
                for d in range(2):
                    if n2 % 2 == 0:
                        last = jnp.where(down == d, n2 // 2, n2 // 2 - 1)
                    else:
                        last = n2 // 2

                    @pl.when((s2 >= 1) & (s2 <= last))
                    def _():
                        src = block(i2 - s2 if d == 0 else i2 + s2, j)
                        base = k * (n2 // 2)
                        ring(src, second_recv.at[d, base + s2 - 1], second[d]).wait_recv()

                        @pl.when(s2 < last)
                        def _():
                            ring(src, second_recv.at[d, base + s2], second[d]).start()

                        to_partner(src)

                return carry

            return lax.fori_loop(0, n1, column, carry)

        lax.fori_loop(0, n1 // 2 + n2 // 2 + 1, step, 0)

    for p in range(CORES):
        pl.when(core == p)(functools.partial(plane, p))

    whole = gath.at[1 - core]
    remote(whole, whole, part_send, part_recv, partner).wait_recv()
    load_l.wait()
    load_c.wait()

    def pieces(zz, y0, count, lo, size):
        return jnp.concatenate(
            [
                gath[c, (zz * ny + y0 + i) if c == 0 else ((y0 + i) * nz + zz), pl.ds(lo, size), :]
                for i in range(count)
                for c in range(CORES)
            ],
            axis=0,
        )

    lad_y = min(ny, 256 // (CORES * pair))
    cyc_y = min(ny, 256 // (CORES * crow))

    def contract(zz, carry):
        lad, cyc = carry
        for y0 in range(0, ny, lad_y):
            width = lad_y * CORES * pair
            start = pl.multiple_of((zz * ny + y0) * CORES * pair, width)
            lad += jnp.dot(
                ladder_v[:, pl.ds(start, width)], pieces(zz, y0, lad_y, 0, pair),
                preferred_element_type=jnp.float32,
            )
        for y0 in range(0, ny, cyc_y):
            width = cyc_y * CORES * crow
            start = pl.multiple_of((zz * ny + y0) * CORES * crow, width)
            cyc += jnp.dot(
                cycle_v[:, pl.ds(start, width)], pieces(zz, y0, cyc_y, pair, crow),
                preferred_element_type=jnp.float32,
            )
        return lad, cyc

    lad, cyc = lax.fori_loop(
        0, nz, contract,
        (jnp.zeros((pair, occ), jnp.float32), jnp.zeros((crow, occ), jnp.float32)),
    )
    mix[...] = cyc.astype(jnp.bfloat16).reshape(nx, cap, occ)
    ret[x] = mix[x]

    def back_x(j):
        to = at(dx=j)
        return remote(mix.at[to[3]], ret.at[x], back_send.at[j], back_recv.at[j], to)

    for j in range(1, nx):
        back_x(j).start()

    sent = gath.at[core, pl.ds(0, blocks - 1)]
    remote(sent, sent, ring_send, first_recv.at[0, 0], partner).wait_send()
    mine = gath.at[core]
    remote(mine, mine, part_send, part_recv, partner).wait_send()
    for j in range(1, nx):
        out_x(j).wait_send()
        back_x(j).wait_recv()
        back_x(j).wait_send()
    term = lax.dot_general(
        onehot, ret[...].reshape(crow, occ), (((0,), (0,)), ((), ())),
        preferred_element_type=jnp.float32,
    )
    out_ref[...] = lad + term


def body(nz, ny, nx, amplitudes, driver, ladder_integrals, cycle_kernel, cycle_target, vir_energy, occ_energy):
    pair, occ = amplitudes.shape
    crow = cycle_kernel.shape[2]
    cap = crow // nx
    blocks = nz * ny
    half = max((ny // 2) * nz, (nz // 2) * ny)
    vmem = pl.BlockSpec(memory_space=pltpu.VMEM)
    hbm = pl.BlockSpec(memory_space=pl.ANY)
    dma = pltpu.SemaphoreType.DMA
    total = pl.pallas_call(
        functools.partial(fused, nz, ny, nx),
        out_shape=jax.ShapeDtypeStruct((pair, occ), jnp.float32),
        in_specs=[vmem, vmem, hbm, hbm],
        out_specs=vmem,
        scratch_shapes=[
            pltpu.VMEM((CORES, blocks, pair + crow, occ), jnp.bfloat16),
            pltpu.VMEM(ladder_integrals.shape[1:], jnp.bfloat16),
            pltpu.VMEM(cycle_kernel.shape[2:], jnp.bfloat16),
            pltpu.VMEM((nx, cap, occ), jnp.bfloat16),
            pltpu.VMEM((nx, cap, occ), jnp.bfloat16),
            pltpu.VMEM((nx, cap, occ), jnp.bfloat16),
            dma((2,)),
            dma,
            dma((2, max(ny, nz) // 2)),
            dma((2, half)),
            dma,
            dma,
            dma((nx,)),
            dma((nx,)),
            dma((nx,)),
            dma((nx,)),
        ],
        compiler_params=pltpu.CompilerParams(collective_id=0, has_side_effects=True),
    )(amplitudes, cycle_target.reshape(1, pair), ladder_integrals[0], cycle_kernel[0, 0])
    denominator = vir_energy[:, None] - occ_energy[None, :]
    return (driver.astype(jnp.float32) + total) / denominator


def solution(mesh, sizes=(12, 8)):
    nz, ny = sizes
    nx = mesh.shape["col"]
    finer = Mesh(mesh.devices.reshape(nz, ny, CORES, nx), ROW_COL)
    in_specs = (
        P(ROW_COL, None),
        P(ROW_COL, None),
        P("col", ROW, None),
        P(ROW, "col", None, None),
        P(ROW_COL),
        P(ROW_COL),
        P(),
    )
    return jax.shard_map(
        functools.partial(body, nz, ny, nx), mesh=finer, in_specs=in_specs,
        out_specs=P(ROW_COL, None), check_vma=False,
    )
```

```python
import functools

import jax
import jax.numpy as jnp
from jax import lax
from jax.experimental import pallas as pl
from jax.experimental.pallas import tpu as pltpu
from jax.sharding import Mesh
from jax.sharding import PartitionSpec as P

ROW = ("row_0", "row_1", "row_2")
ROW_COL = ("row_0", "row_1", "row_2", "col")
MESH = pl.DeviceIdType.MESH
CORES = 2
CHUNKS = 4
AXIS = ("dy", "dz")


def fused(
    nz, ny, nx, amp_ref, tgt_ref, ladder_hbm, cycle_hbm, out_ref,
    gath, ladder_v, cycle_v, placed, mix, ret,
    w_sem, ring_send, first_recv, second_recv, part_send, part_recv,
    a_send, t_send, x_recv, back_send, back_recv,
):
    z, y, core, x = (lax.axis_index(a) for a in ROW_COL)
    pair, occ = amp_ref.shape
    cap = placed.shape[1]
    crow = nx * cap
    blocks = nz * ny

    load_l = pltpu.make_async_copy(ladder_hbm, ladder_v, w_sem.at[0])
    load_c = pltpu.make_async_copy(cycle_hbm, cycle_v, w_sem.at[1])
    load_l.start()
    load_c.start()

    def at(dz=0, dy=0, dx=0, dc=0):
        return (
            lax.rem(z + dz + nz, nz), lax.rem(y + dy + ny, ny),
            lax.rem(core + dc, CORES), lax.rem(x + dx, nx),
        )

    barrier = pltpu.get_barrier_semaphore()

    def greet(peers):
        for peer in peers:
            pl.semaphore_signal(barrier, inc=1, device_id=peer, device_id_type=MESH)

    def peers_of(p):
        n1 = ny if p == 0 else nz
        along = [at(dx=j, **{AXIS[p]: o}) for o in range(n1) for j in range(nx) if o or j]
        across = [at(**{AXIS[1 - p]: d}) for d in (1, -1)]
        return along + across + [at(dc=1)]

    for p in range(CORES):

        @pl.when(core == p)
        def _():
            greet(peers_of(p))

    slot_ids = lax.broadcasted_iota(jnp.int32, (crow, pair), 0)
    onehot = (slot_ids == tgt_ref[...]).astype(jnp.float32).astype(jnp.bfloat16)
    own = jnp.dot(onehot, amp_ref[...], preferred_element_type=jnp.float32)
    placed[...] = own.astype(jnp.bfloat16).reshape(nx, cap, occ)

    my_slot = jnp.where(core == 0, z * ny + y, y * nz + z)
    gath[core, my_slot, pl.ds(0, pair), :] = amp_ref[...]
    my_part = pl.ds(pl.multiple_of(pair + x * cap, cap), cap)
    gath[core, my_slot, my_part, :] = placed[x]

    for p in range(CORES):

        @pl.when(core == p)
        def _():
            pl.semaphore_wait(barrier, len(peers_of(p)))

    def remote(src, dst, send_sem, recv_sem, device):
        return pltpu.make_async_remote_copy(
            src_ref=src, dst_ref=dst, send_sem=send_sem, recv_sem=recv_sem,
            device_id=device, device_id_type=MESH,
        )

    partner = at(dc=1)

    def plane(p):
        n1, n2 = (ny, nz) if p == 0 else (nz, ny)
        i1, i2 = (y, z) if p == 0 else (z, y)
        second = [at(**{AXIS[1 - p]: d}) for d in (1, -1)]
        size = n1 // CHUNKS
        home = i1 // size
        r2 = n2 // 2
        across = [lax.rem(i2 + d + n2, n2) for d in range(-r2, r2 + 1)]
        order = [lax.rem(home + (j + 1) // 2 * (1 if j % 2 else CHUNKS - 1), CHUNKS) for j in range(CHUNKS)]

        hops = sorted(range(n1), key=lambda o: -min(o, n1 - o))
        for o in hops:
            for j in sorted(range(nx), key=lambda j: -min(j, nx - j)):
                if o or j:
                    to = at(dx=j, **{AXIS[p]: o})
                    remote(
                        placed.at[to[3]], gath.at[p, my_slot, my_part, :], t_send,
                        first_recv.at[home] if o else x_recv, to,
                    ).start()
            if o:
                mine = gath.at[p, my_slot, pl.ds(0, pair), :]
                remote(mine, mine, a_send, first_recv.at[home], at(**{AXIS[p]: o})).start()

        def chunk(d2, j, count=size):
            return gath.at[p, pl.ds(across[r2 + d2] * n1 + order[j] * size, count)]

        def ring(src, recv_sem, device):
            return remote(src, src, ring_send, recv_sem, device)

        def to_partner(src):
            remote(src, src, part_send, part_recv, partner).start()

        for j in range(CHUNKS):
            if j == 0:
                rest = gath.at[p, my_slot, pl.ds(0, (nx - 1) * cap), :]
                remote(rest, rest, t_send, x_recv, partner).wait_recv()
            got = chunk(0, j, size if j else size - 1)
            ring(got, first_recv.at[order[j]], partner).wait_recv()
            src = chunk(0, j)
            for d in range(2):
                ring(src, second_recv.at[d, j * r2], second[d]).start()
            to_partner(src)

        for s in range(1, r2 + 1):
            for j in range(CHUNKS):
                for d in range(2):
                    last = r2 - (n2 % 2 == 0 and j % 2 != d)
                    if s <= last:
                        src = chunk(s if d else -s, j)
                        ring(src, second_recv.at[d, j * r2 + s - 1], second[d]).wait_recv()
                        if s < last:
                            ring(src, second_recv.at[d, j * r2 + s], second[d]).start()
                        to_partner(src)

        sent = gath.at[p, pl.ds(0, n1 * (n2 - 1))]
        ring(sent, x_recv, partner).wait_send()
        a_all = gath.at[p, pl.ds(0, n1 - 1), pl.ds(0, pair), :]
        remote(a_all, a_all, a_send, x_recv, partner).wait_send()
        t_all = gath.at[p, pl.ds(0, n1 * nx - 1), pl.ds(0, cap), :]
        remote(t_all, t_all, t_send, x_recv, partner).wait_send()

    for p in range(CORES):
        pl.when(core == p)(functools.partial(plane, p))

    whole = gath.at[1 - core]
    remote(whole, whole, part_send, part_recv, partner).wait_recv()
    load_l.wait()
    load_c.wait()

    def pieces(zz, y0, count, lo, size):
        return jnp.concatenate(
            [
                gath[c, (zz * ny + y0 + i) if c == 0 else ((y0 + i) * nz + zz), pl.ds(lo, size), :]
                for i in range(count)
                for c in range(CORES)
            ],
            axis=0,
        )

    lad_y = min(ny, 256 // (CORES * pair))
    cyc_y = min(ny, 256 // (CORES * crow))

    def contract(zz, carry):
        lad, cyc = carry
        for y0 in range(0, ny, lad_y):
            width = lad_y * CORES * pair
            start = pl.multiple_of((zz * ny + y0) * CORES * pair, width)
            lad += jnp.dot(
                ladder_v[:, pl.ds(start, width)], pieces(zz, y0, lad_y, 0, pair),
                preferred_element_type=jnp.float32,
            )
        for y0 in range(0, ny, cyc_y):
            width = cyc_y * CORES * crow
            start = pl.multiple_of((zz * ny + y0) * CORES * crow, width)
            cyc += jnp.dot(
                cycle_v[:, pl.ds(start, width)], pieces(zz, y0, cyc_y, pair, crow),
                preferred_element_type=jnp.float32,
            )
        return lad, cyc

    lad, cyc = lax.fori_loop(
        0, nz, contract,
        (jnp.zeros((pair, occ), jnp.float32), jnp.zeros((crow, occ), jnp.float32)),
    )
    mix[...] = cyc.astype(jnp.bfloat16).reshape(nx, cap, occ)
    ret[x] = mix[x]

    def back_x(j):
        to = at(dx=j)
        return remote(mix.at[to[3]], ret.at[x], back_send.at[j], back_recv.at[j], to)

    for j in range(1, nx):
        back_x(j).start()

    mine = gath.at[core]
    remote(mine, mine, part_send, part_recv, partner).wait_send()
    for j in range(1, nx):
        back_x(j).wait_recv()
        back_x(j).wait_send()
    term = lax.dot_general(
        onehot, ret[...].reshape(crow, occ), (((0,), (0,)), ((), ())),
        preferred_element_type=jnp.float32,
    )
    out_ref[...] = lad + term


def body(nz, ny, nx, amplitudes, driver, ladder_integrals, cycle_kernel, cycle_target, vir_energy, occ_energy):
    pair, occ = amplitudes.shape
    crow = cycle_kernel.shape[2]
    cap = crow // nx
    blocks = nz * ny
    vmem = pl.BlockSpec(memory_space=pltpu.VMEM)
    hbm = pl.BlockSpec(memory_space=pl.ANY)
    dma = pltpu.SemaphoreType.DMA
    total = pl.pallas_call(
        functools.partial(fused, nz, ny, nx),
        out_shape=jax.ShapeDtypeStruct((pair, occ), jnp.float32),
        in_specs=[vmem, vmem, hbm, hbm],
        out_specs=vmem,
        scratch_shapes=[
            pltpu.VMEM((CORES, blocks, pair + crow, occ), jnp.bfloat16),
            pltpu.VMEM(ladder_integrals.shape[1:], jnp.bfloat16),
            pltpu.VMEM(cycle_kernel.shape[2:], jnp.bfloat16),
            pltpu.VMEM((nx, cap, occ), jnp.bfloat16),
            pltpu.VMEM((nx, cap, occ), jnp.bfloat16),
            pltpu.VMEM((nx, cap, occ), jnp.bfloat16),
            dma((2,)),
            dma,
            dma((CHUNKS,)),
            dma((2, CHUNKS * (max(ny, nz) // 2))),
            dma,
            dma,
            dma,
            dma,
            dma,
            dma((nx,)),
            dma((nx,)),
        ],
        compiler_params=pltpu.CompilerParams(collective_id=0, has_side_effects=True),
    )(amplitudes, cycle_target.reshape(1, pair), ladder_integrals[0], cycle_kernel[0, 0])
    denominator = vir_energy[:, None] - occ_energy[None, :]
    return (driver.astype(jnp.float32) + total) / denominator


def solution(mesh, sizes=(12, 8)):
    nz, ny = sizes
    nx = mesh.shape["col"]
    finer = Mesh(mesh.devices.reshape(nz, ny, CORES, nx), ROW_COL)
    in_specs = (
        P(ROW_COL, None),
        P(ROW_COL, None),
        P("col", ROW, None),
        P(ROW, "col", None, None),
        P(ROW_COL),
        P(ROW_COL),
        P(),
    )
    return jax.shard_map(
        functools.partial(body, nz, ny, nx), mesh=finer, in_specs=in_specs,
        out_specs=P(ROW_COL, None), check_vma=False,
    )
```

```python
import functools

import jax
import jax.numpy as jnp
from jax import lax
from jax.experimental import pallas as pl
from jax.experimental.pallas import tpu as pltpu
from jax.sharding import Mesh
from jax.sharding import PartitionSpec as P

ROW = ("row_0", "row_1", "row_2")
ROW_COL = ("row_0", "row_1", "row_2", "col")
MESH = pl.DeviceIdType.MESH
CORES = 2
CHUNKS = (4, 4)
SKIP = (2, 2)


def fused(
    nz, ny, nx, amp_ref, tgt_ref, ladder_hbm, cycle_hbm, out_ref,
    gath, ladder_v, cycle_v, placed, mix, ret,
    w_sem, first_send, first_recv, ring_send, ring_recv, part_send, part_recv,
    x_send, x_recv, back_send, back_recv,
):
    z, y, core, x = (lax.axis_index(a) for a in ROW_COL)
    pair, occ = amp_ref.shape
    cap = placed.shape[1]
    crow = nx * cap
    blocks = nz * ny
    half = (pair + crow) // 2
    here = (half - pair) // cap

    def at(dz=0, dy=0, dx=0, dc=0):
        return (
            lax.rem(z + dz + nz, nz), lax.rem(y + dy + ny, ny),
            lax.rem(core + dc, CORES), lax.rem(x + dx, nx),
        )

    barrier = pltpu.get_barrier_semaphore()
    peers = [at(dz=o) for o in range(1, nz)] + [at(dy=o) for o in range(1, ny)]
    peers += [at(dx=j) for j in range(1, nx)] + [at(dc=1)]
    for peer in peers:
        pl.semaphore_signal(barrier, inc=1, device_id=peer, device_id_type=MESH)
    load_l = pltpu.make_async_copy(ladder_hbm, ladder_v, w_sem.at[0])
    load_c = pltpu.make_async_copy(cycle_hbm, cycle_v, w_sem.at[1])
    load_l.start()
    load_c.start()

    slot_ids = lax.broadcasted_iota(jnp.int32, (crow, pair), 0)
    onehot = (slot_ids == tgt_ref[...]).astype(jnp.float32).astype(jnp.bfloat16)
    own = jnp.dot(onehot, amp_ref[...], preferred_element_type=jnp.float32)
    placed[...] = own.astype(jnp.bfloat16).reshape(nx, cap, occ)

    slots = [z * ny + y, y * nz + z]
    gath[0, core, slots[0], pl.ds(0, pair), :] = amp_ref[...]
    in_first = x < here
    my_half = jnp.where(in_first, 0, 1)
    my_slot = jnp.where(in_first, slots[0], slots[1])
    my_row = pl.multiple_of(jnp.where(in_first, pair + x * cap, (x - here) * cap), cap)
    gath[my_half, core, my_slot, pl.ds(my_row, cap), :] = placed[x]

    pl.semaphore_wait(barrier, len(peers))

    def remote(src, dst, send_sem, recv_sem, device):
        return pltpu.make_async_remote_copy(
            src_ref=src, dst_ref=dst, send_sem=send_sem, recv_sem=recv_sem,
            device_id=device, device_id_type=MESH,
        )

    def same(src, send_sem, recv_sem, device):
        return remote(src, src, send_sem, recv_sem, device)

    def out_x(j):
        to = at(dx=j)
        part = gath.at[my_half, core, my_slot, pl.ds(my_row, cap), :]
        return remote(placed.at[to[3]], part, x_send.at[j], x_recv.at[j], to)

    for j in range(1, nx):
        out_x(j).start()
    for j in range(1, nx):
        out_x(j).wait_recv()

    partner = at(dc=1)

    def plane(p):
        n1, n2 = (ny, nz) if p == 0 else (nz, ny)
        i1, i2 = (y, z) if p == 0 else (z, y)
        along, across = ("dy", "dz") if p == 0 else ("dz", "dy")
        second = [[at(**{across: d * k}) for k in (1, 2)] for d in (1, -1)]
        skip = SKIP[p]
        chunks = CHUNKS[p]
        size = n1 // chunks
        reach = n2 // 2
        home = i1 // size
        order = [
            lax.rem(home + (j + 1) // 2 * (1 if j % 2 else chunks - 1), chunks) for j in range(chunks)
        ]

        def chunk(d2, j, count=size):
            a2 = lax.rem(i2 + d2 + n2, n2)
            return gath.at[p, core, pl.ds(a2 * n1 + order[j] * size, count)]

        def hop(src, j, d, s, far=1):
            arrives = ring_recv.at[p, d, j * reach + s + far - 1]
            return same(src, ring_send.at[p], arrives, second[d][far - 1])

        def send_on(src, j, d, s):
            if s % skip == 0:
                for far in range(skip, 0, -1):
                    if s + far <= last(j, d):
                        hop(src, j, d, s, far).start()

        def last(j, d):
            return reach - (n2 % 2 == 0 and j % 2 != d)

        def to_partner(src):
            same(src, part_send, part_recv, partner).start()

        def begin():
            mine = gath.at[p, core, slots[p]]
            for o in sorted(range(1, n1), key=lambda o: -min(o, n1 - o)):
                same(mine, first_send.at[p], first_recv.at[p, home], at(**{along: o})).start()

        def launch():
            for j in range(chunks):
                if size > (j == 0):
                    got = chunk(0, j, size - (j == 0))
                    same(got, first_send.at[p], first_recv.at[p, order[j]], partner).wait_recv()
                src = chunk(0, j)
                for d in range(2):
                    send_on(src, j, d, 0)
                to_partner(src)

        def step(s):
            for j in range(chunks):
                for d in range(2):
                    if s <= last(j, d):
                        src = chunk(s if d else -s, j)
                        hop(src, j, d, s - 1).wait_recv()
                        send_on(src, j, d, s)
                        to_partner(src)

        def finish():
            sent = gath.at[p, core, pl.ds(0, n1 * (n2 - 1))]
            same(sent, ring_send.at[p], part_recv, partner).wait_send()
            sent = gath.at[p, core, pl.ds(0, n1 - 1)]
            same(sent, first_send.at[p], part_recv, partner).wait_send()

        return begin, launch, step, finish, reach

    planes = [plane(p) for p in range(2)]
    for p in (1, 0):
        planes[p][0]()
    for p in (0, 1):
        planes[p][1]()
    lists = [sorted(range(1, r[4] + 1), key=lambda s: (-(-s // k), s % k)) for r, k in zip(planes, SKIP)]
    for i in range(max(nz, ny) // 2):
        for p in (0, 1):
            if i < len(lists[p]):
                planes[p][2](lists[p][i])

    whole = gath.at[:, 1 - core]
    same(whole, part_send, part_recv, partner).wait_recv()
    load_l.wait()
    load_c.wait()

    def pieces(zz, y0, count, parts):
        rows = []
        for i in range(count):
            for c in range(CORES):
                for p, lo, n in parts:
                    slot = zz * ny + y0 + i if p == 0 else (y0 + i) * nz + zz
                    if n:
                        rows.append(gath[p, c, slot, pl.ds(lo, n), :])
        return jnp.concatenate(rows, axis=0)

    lad_parts = [(0, 0, pair)]
    cyc_parts = [(0, pair, half - pair), (1, 0, half)]
    lad_y = min(ny, 256 // (CORES * pair))
    cyc_y = min(ny, 256 // (CORES * crow))

    def contract(zz, carry):
        lad, cyc = carry
        for y0 in range(0, ny, lad_y):
            width = lad_y * CORES * pair
            start = pl.multiple_of((zz * ny + y0) * CORES * pair, width)
            lad += jnp.dot(
                ladder_v[:, pl.ds(start, width)], pieces(zz, y0, lad_y, lad_parts),
                preferred_element_type=jnp.float32,
            )
        for y0 in range(0, ny, cyc_y):
            width = cyc_y * CORES * crow
            start = pl.multiple_of((zz * ny + y0) * CORES * crow, width)
            cyc += jnp.dot(
                cycle_v[:, pl.ds(start, width)], pieces(zz, y0, cyc_y, cyc_parts),
                preferred_element_type=jnp.float32,
            )
        return lad, cyc

    lad, cyc = lax.fori_loop(
        0, nz, contract,
        (jnp.zeros((pair, occ), jnp.float32), jnp.zeros((crow, occ), jnp.float32)),
        unroll=3,
    )
    mix[...] = cyc.astype(jnp.bfloat16).reshape(nx, cap, occ)
    ret[x] = mix[x]

    def back_x(j):
        to = at(dx=j)
        return remote(mix.at[to[3]], ret.at[x], back_send.at[j], back_recv.at[j], to)

    for j in range(1, nx):
        back_x(j).start()
    for p in range(2):
        planes[p][3]()
    every = gath.at[:, core]
    same(every, part_send, part_recv, partner).wait_send()
    for j in range(1, nx):
        out_x(j).wait_send()
        back_x(j).wait_recv()
        back_x(j).wait_send()
    term = lax.dot_general(
        onehot, ret[...].reshape(crow, occ), (((0,), (0,)), ((), ())),
        preferred_element_type=jnp.float32,
    )
    out_ref[...] = lad + term


def body(nz, ny, nx, amplitudes, driver, ladder_integrals, cycle_kernel, cycle_target, vir_energy, occ_energy):
    pair, occ = amplitudes.shape
    crow = cycle_kernel.shape[2]
    cap = crow // nx
    blocks = nz * ny
    half = (pair + crow) // 2
    vmem = pl.BlockSpec(memory_space=pltpu.VMEM)
    hbm = pl.BlockSpec(memory_space=pl.ANY)
    dma = pltpu.SemaphoreType.DMA
    total = pl.pallas_call(
        functools.partial(fused, nz, ny, nx),
        out_shape=jax.ShapeDtypeStruct((pair, occ), jnp.float32),
        in_specs=[vmem, vmem, hbm, hbm],
        out_specs=vmem,
        scratch_shapes=[
            pltpu.VMEM((2, CORES, blocks, half, occ), jnp.bfloat16),
            pltpu.VMEM(ladder_integrals.shape[1:], jnp.bfloat16),
            pltpu.VMEM(cycle_kernel.shape[2:], jnp.bfloat16),
            pltpu.VMEM((nx, cap, occ), jnp.bfloat16),
            pltpu.VMEM((nx, cap, occ), jnp.bfloat16),
            pltpu.VMEM((nx, cap, occ), jnp.bfloat16),
            dma((2,)),
            dma((2,)),
            dma((2, max(CHUNKS))),
            dma((2,)),
            dma((2, 2, max(CHUNKS) * (max(ny, nz) // 2))),
            dma,
            dma,
            dma((nx,)),
            dma((nx,)),
            dma((nx,)),
            dma((nx,)),
        ],
        compiler_params=pltpu.CompilerParams(collective_id=0, has_side_effects=True),
    )(amplitudes, cycle_target.reshape(1, pair), ladder_integrals[0], cycle_kernel[0, 0])
    denominator = vir_energy[:, None] - occ_energy[None, :]
    return (driver.astype(jnp.float32) + total) / denominator


def solution(mesh, sizes=(12, 8)):
    nz, ny = sizes
    nx = mesh.shape["col"]
    finer = Mesh(mesh.devices.reshape(nz, ny, CORES, nx), ROW_COL)
    in_specs = (
        P(ROW_COL, None),
        P(ROW_COL, None),
        P("col", ROW, None),
        P(ROW, "col", None, None),
        P(ROW_COL),
        P(ROW_COL),
        P(),
    )
    return jax.shard_map(
        functools.partial(body, nz, ny, nx), mesh=finer, in_specs=in_specs,
        out_specs=P(ROW_COL, None), check_vma=False,
    )
```

```python
import functools

import jax
import jax.numpy as jnp
from jax import lax
from jax.experimental import pallas as pl
from jax.experimental.pallas import tpu as pltpu
from jax.sharding import Mesh
from jax.sharding import PartitionSpec as P

ROW = ("row_0", "row_1", "row_2")
ROW_COL = ("row_0", "row_1", "row_2", "col")
MESH = pl.DeviceIdType.MESH
CORES = 2
CHUNKS = (4, 4)
SKIP = (2, 2)


def fused(
    nz, ny, nx, amp_ref, tgt_ref, ladder_hbm, cycle_hbm, out_ref,
    gath, ladder_v, cycle_v, placed, mix, ret,
    w_sem, first_send, first_recv, ring_send, ring_recv, part_send, part_recv,
    x_send, x_recv, back_send, back_recv,
):
    z, y, core, x = (lax.axis_index(a) for a in ROW_COL)
    pair, occ = amp_ref.shape
    cap = placed.shape[1]
    crow = nx * cap
    blocks = nz * ny
    half = (pair + crow) // 2
    here = (half - pair) // cap

    def at(dz=0, dy=0, dx=0, dc=0):
        return (
            lax.rem(z + dz + nz, nz), lax.rem(y + dy + ny, ny),
            lax.rem(core + dc, CORES), lax.rem(x + dx, nx),
        )

    barrier = pltpu.get_barrier_semaphore()
    peers = [at(dz=o) for o in range(1, nz)] + [at(dy=o) for o in range(1, ny)]
    peers += [at(dx=j) for j in range(1, nx)] + [at(dc=1)]
    for peer in peers:
        pl.semaphore_signal(barrier, inc=1, device_id=peer, device_id_type=MESH)
    load_l = pltpu.make_async_copy(ladder_hbm, ladder_v, w_sem.at[0])
    load_c = pltpu.make_async_copy(cycle_hbm, cycle_v, w_sem.at[1])
    load_l.start()
    load_c.start()

    slot_ids = lax.broadcasted_iota(jnp.int32, (crow, pair), 0)
    onehot = (slot_ids == tgt_ref[...]).astype(jnp.float32).astype(jnp.bfloat16)
    own = jnp.dot(onehot, amp_ref[...], preferred_element_type=jnp.float32)
    placed[...] = own.astype(jnp.bfloat16).reshape(nx, cap, occ)

    slots = [z * ny + y, y * nz + z]
    gath[0, core, slots[0], pl.ds(0, pair), :] = amp_ref[...]
    in_first = x < here
    my_half = jnp.where(in_first, 0, 1)
    my_slot = jnp.where(in_first, slots[0], slots[1])
    my_row = pl.multiple_of(jnp.where(in_first, pair + x * cap, (x - here) * cap), cap)
    gath[my_half, core, my_slot, pl.ds(my_row, cap), :] = placed[x]

    pl.semaphore_wait(barrier, len(peers))

    def remote(src, dst, send_sem, recv_sem, device):
        return pltpu.make_async_remote_copy(
            src_ref=src, dst_ref=dst, send_sem=send_sem, recv_sem=recv_sem,
            device_id=device, device_id_type=MESH,
        )

    def same(src, send_sem, recv_sem, device):
        return remote(src, src, send_sem, recv_sem, device)

    def out_x(j):
        to = at(dx=j)
        part = gath.at[my_half, core, my_slot, pl.ds(my_row, cap), :]
        return remote(placed.at[to[3]], part, x_send.at[j], x_recv.at[j], to)

    for j in range(1, nx):
        out_x(j).start()
    for j in range(1, nx):
        out_x(j).wait_recv()

    partner = at(dc=1)

    def plane(p):
        n1, n2 = (ny, nz) if p == 0 else (nz, ny)
        i1, i2 = (y, z) if p == 0 else (z, y)
        along, across = ("dy", "dz") if p == 0 else ("dz", "dy")
        second = [[at(**{across: d * k}) for k in (1, 2)] for d in (1, -1)]
        skip = SKIP[p]
        chunks = CHUNKS[p]
        size = n1 // chunks
        reach = n2 // 2
        home = i1 // size
        order = [
            lax.rem(home + (j + 1) // 2 * (1 if j % 2 else chunks - 1), chunks) for j in range(chunks)
        ]

        def chunk(d2, j, count=size):
            a2 = lax.rem(i2 + d2 + n2, n2)
            return gath.at[p, core, pl.ds(a2 * n1 + order[j] * size, count)]

        def hop(src, j, d, s, far=1):
            arrives = ring_recv.at[p, d, j * reach + s + far - 1]
            return same(src, ring_send.at[p], arrives, second[d][far - 1])

        def send_on(src, j, d, s):
            if s % skip == 0:
                for far in range(skip, 0, -1):
                    if s + far <= last(j, d):
                        hop(src, j, d, s, far).start()

        def last(j, d):
            return reach - (n2 % 2 == 0 and j % 2 != d)

        def to_partner(src):
            same(src, part_send, part_recv, partner).start()

        def begin():
            mine = gath.at[p, core, slots[p]]
            for o in sorted(range(1, n1), key=lambda o: -min(o, n1 - o)):
                same(mine, first_send.at[p], first_recv.at[p, home], at(**{along: o})).start()

        def launch():
            for j in range(chunks):
                if size > (j == 0):
                    got = chunk(0, j, size - (j == 0))
                    same(got, first_send.at[p], first_recv.at[p, order[j]], partner).wait_recv()
                src = chunk(0, j)
                for d in range(2):
                    send_on(src, j, d, 0)
                to_partner(src)

        def step(s):
            for j in range(chunks):
                for d in range(2):
                    if s <= last(j, d):
                        src = chunk(s if d else -s, j)
                        hop(src, j, d, s - 1).wait_recv()
                        send_on(src, j, d, s)
                        to_partner(src)

        def finish():
            sent = gath.at[p, core, pl.ds(0, n1 * (n2 - 1))]
            same(sent, ring_send.at[p], part_recv, partner).wait_send()
            sent = gath.at[p, core, pl.ds(0, n1 - 1)]
            same(sent, first_send.at[p], part_recv, partner).wait_send()

        return begin, launch, step, finish, reach

    planes = [plane(p) for p in range(2)]
    for p in (1, 0):
        planes[p][0]()
    for p in (0, 1):
        planes[p][1]()
    lists = [sorted(range(1, r[4] + 1), key=lambda s: (-(-s // k), s % k)) for r, k in zip(planes, SKIP)]
    for i in range(max(nz, ny) // 2):
        for p in (0, 1):
            if i < len(lists[p]):
                planes[p][2](lists[p][i])

    whole = gath.at[:, 1 - core]
    same(whole, part_send, part_recv, partner).wait_recv()
    load_l.wait()
    load_c.wait()

    def pieces(zz, y0, count, parts):
        rows = []
        for i in range(count):
            for c in range(CORES):
                for p, lo, n in parts:
                    slot = zz * ny + y0 + i if p == 0 else (y0 + i) * nz + zz
                    if n:
                        rows.append(gath[p, c, slot, pl.ds(lo, n), :])
        return jnp.concatenate(rows, axis=0)

    lad_parts = [(0, 0, pair)]
    cyc_parts = [(0, pair, half - pair), (1, 0, half)]
    lad_y = min(ny, 256 // (CORES * pair))
    cyc_y = min(ny, 256 // (CORES * crow))

    def ladder_sum(zz, lad):
        for y0 in range(0, ny, lad_y):
            width = lad_y * CORES * pair
            start = pl.multiple_of((zz * ny + y0) * CORES * pair, width)
            lad += jnp.dot(
                ladder_v[:, pl.ds(start, width)], pieces(zz, y0, lad_y, lad_parts),
                preferred_element_type=jnp.float32,
            )
        return lad

    def cycle_sum(zz, cyc):
        for y0 in range(0, ny, cyc_y):
            width = cyc_y * CORES * crow
            start = pl.multiple_of((zz * ny + y0) * CORES * crow, width)
            cyc += jnp.dot(
                cycle_v[:, pl.ds(start, width)], pieces(zz, y0, cyc_y, cyc_parts),
                preferred_element_type=jnp.float32,
            )
        return cyc

    cyc = lax.fori_loop(0, nz, cycle_sum, jnp.zeros((crow, occ), jnp.float32), unroll=3)
    mix[...] = cyc.astype(jnp.bfloat16).reshape(nx, cap, occ)
    ret[x] = mix[x]

    def back_x(j):
        to = at(dx=j)
        return remote(mix.at[to[3]], ret.at[x], back_send.at[j], back_recv.at[j], to)

    for j in range(1, nx):
        back_x(j).start()
    lad = lax.fori_loop(0, nz, ladder_sum, jnp.zeros((pair, occ), jnp.float32), unroll=3)
    for p in range(2):
        planes[p][3]()
    every = gath.at[:, core]
    same(every, part_send, part_recv, partner).wait_send()
    for j in range(1, nx):
        out_x(j).wait_send()
        back_x(j).wait_recv()
        back_x(j).wait_send()
    term = lax.dot_general(
        onehot, ret[...].reshape(crow, occ), (((0,), (0,)), ((), ())),
        preferred_element_type=jnp.float32,
    )
    out_ref[...] = lad + term


def body(nz, ny, nx, amplitudes, driver, ladder_integrals, cycle_kernel, cycle_target, vir_energy, occ_energy):
    pair, occ = amplitudes.shape
    crow = cycle_kernel.shape[2]
    cap = crow // nx
    blocks = nz * ny
    half = (pair + crow) // 2
    vmem = pl.BlockSpec(memory_space=pltpu.VMEM)
    hbm = pl.BlockSpec(memory_space=pl.ANY)
    dma = pltpu.SemaphoreType.DMA
    total = pl.pallas_call(
        functools.partial(fused, nz, ny, nx),
        out_shape=jax.ShapeDtypeStruct((pair, occ), jnp.float32),
        in_specs=[vmem, vmem, hbm, hbm],
        out_specs=vmem,
        scratch_shapes=[
            pltpu.VMEM((2, CORES, blocks, half, occ), jnp.bfloat16),
            pltpu.VMEM(ladder_integrals.shape[1:], jnp.bfloat16),
            pltpu.VMEM(cycle_kernel.shape[2:], jnp.bfloat16),
            pltpu.VMEM((nx, cap, occ), jnp.bfloat16),
            pltpu.VMEM((nx, cap, occ), jnp.bfloat16),
            pltpu.VMEM((nx, cap, occ), jnp.bfloat16),
            dma((2,)),
            dma((2,)),
            dma((2, max(CHUNKS))),
            dma((2,)),
            dma((2, 2, max(CHUNKS) * (max(ny, nz) // 2))),
            dma,
            dma,
            dma((nx,)),
            dma((nx,)),
            dma((nx,)),
            dma((nx,)),
        ],
        compiler_params=pltpu.CompilerParams(collective_id=0, has_side_effects=True),
    )(amplitudes, cycle_target.reshape(1, pair), ladder_integrals[0], cycle_kernel[0, 0])
    denominator = vir_energy[:, None] - occ_energy[None, :]
    return (driver.astype(jnp.float32) + total) / denominator


def solution(mesh, sizes=(12, 8)):
    nz, ny = sizes
    nx = mesh.shape["col"]
    finer = Mesh(mesh.devices.reshape(nz, ny, CORES, nx), ROW_COL)
    in_specs = (
        P(ROW_COL, None),
        P(ROW_COL, None),
        P("col", ROW, None),
        P(ROW, "col", None, None),
        P(ROW_COL),
        P(ROW_COL),
        P(),
    )
    return jax.shard_map(
        functools.partial(body, nz, ny, nx), mesh=finer, in_specs=in_specs,
        out_specs=P(ROW_COL, None), check_vma=False,
    )
```
